32 devices in a mesh: groups: 1, wide: 16 (over z, y, core), tp: 2 (over x), sub: 1.
Axes of the slice: x: 2, y: 2, z: 4, core: 2. Of those that a mesh axis runs over, the one named last changes fastest.
Arguments:
- moe_input: bfloat16 [128, 3584], P(('groups', 'wide', 'tp', 'sub')), may hold values from -6 to 6
- routes: int32 [128, 8], P(('groups', 'wide', 'tp', 'sub')), may hold values from 0 to 15, all different within a row; in each aligned block of 4 rows (0 to 3, 4 to 7, ...) at most 4 rows name the same one
- router_weight: bfloat16 [3584, 16], replicated, may hold values from -0.1875 to 0.1875
- gate_weight: bfloat16 [16, 3584, 1024], P('wide', None, ('tp', 'sub')), may hold values from -0.09375 to 0.09375
- up_weight: bfloat16 [16, 3584, 1024], P('wide', None, ('tp', 'sub')), may hold values from -0.09375 to 0.09375
- down_weight: bfloat16 [16, 1024, 3584], P('wide', ('tp', 'sub')), may hold values from -0.1875 to 0.1875
- query_latent: bfloat16 [16, 128, 512], P(('groups', 'wide', 'sub')), may hold values from -20 to 20
- query_rope: bfloat16 [16, 64, 128], P(('groups', 'wide', 'sub')), may hold values from -6 to 6
- cache_latent: bfloat16 [16, 4096, 512], P(('groups', 'wide', 'sub'), 'tp'), may hold values from -6 to 6
- cache_rope: bfloat16 [16, 64, 4096], P(('groups', 'wide', 'sub'), None, 'tp'), may hold values from -6 to 6
- cache_lengths: int32 [16], P(('groups', 'wide', 'sub')), may hold values from 256 to 4096, as said below
Outputs:
- moe_out: bfloat16 [128, 3584], P(('groups', 'wide', 'tp', 'sub'))
- att_out: bfloat16 [16, 128, 512], P(('groups', 'wide', 'sub'))
The draws below stay inside these ranges and needn't reach their ends.
Inputs may be any that keep to these rules, and one draw needn't show every extreme that they name: `routes`: within the 4 rows of one device no expert is named by more than 4 rows, and in some device's rows an expert is named by exactly 4 of them. Row r attends to its cached positions 0 to cache_lengths[r] - 1; in every draw some row has exactly 4096.
All inputs are finite; a program needn't handle non-finite values.
Results may differ from the reference program's by a relative error of at most 0.015.
Values may be sent and summed in bfloat16 or wider, within the bound.
No kernel may reach another device: no remote copies, remote signals or barrier semaphores. Data moves between devices by JAX's collectives and lax.ppermute only.
A program may use at most 64 MiB of HBM per device.

```python
import math
import jax
import jax.numpy as jnp
import numpy as np
from jax import lax

D = 3584
FF = 1024
EXPERTS = 16
TOPK = 8
MOE_DEV = 4
CAP = 4
MOE_ROWS = 128
HEADS = 128
KV_LAT = 512
ROPE = 64
LEN = 4096
ATT_ROWS = 16
N_TP = 2
N_SUB = 1


def lengths_table(key):
    seeded = jax.random.fold_in(key, 11)
    first_key, second_key = jax.random.split(seeded)
    drawn = jax.random.randint(first_key, (ATT_ROWS,), LEN // 16, LEN + 1, dtype=jnp.int32)
    longest = jax.random.randint(second_key, (), 0, ATT_ROWS, dtype=jnp.int32)
    return jnp.where(jnp.arange(ATT_ROWS, dtype=jnp.int32) == longest, LEN, drawn)


def latent_table(key):
    lengths = lengths_table(key)
    seeded = jax.random.fold_in(key, 23)
    first_key, second_key = jax.random.split(seeded)
    base = jnp.clip(jax.random.normal(first_key, (ATT_ROWS, LEN, KV_LAT), jnp.float32), -6.0, 6.0)
    signs = jnp.where(jax.random.bernoulli(second_key, 0.5, (ATT_ROWS, KV_LAT)), 1.0, -1.0).astype(jnp.float32)
    entry_ids = jnp.arange(KV_LAT, dtype=jnp.int32)
    alternate = jnp.where(entry_ids % 2 == 0, 1.0, -1.0).astype(jnp.float32)
    lowered = jnp.where(entry_ids == 1, 2.0, 0.0).astype(jnp.float32)
    newest = 5.0 * signs
    twin = signs * (5.0 + alternate[None, :] - lowered[None, :])
    row_ids = jnp.arange(ATT_ROWS, dtype=jnp.int32)
    base = base.at[row_ids, lengths - 1].set(newest)
    base = base.at[row_ids, lengths // 2].set(twin)
    return (base, signs)


def draw_cache_lengths(key, part):
    return lengths_table(key)


def draw_cache_latent(key, part):
    return latent_table(key)[0].astype(jnp.bfloat16)


def draw_query_latent(key, part):
    table, signs = latent_table(key)
    seeded = jax.random.fold_in(key, 37)
    first_key, second_key = jax.random.split(seeded)
    noise = jnp.clip(jax.random.normal(first_key, (ATT_ROWS, HEADS, KV_LAT), jnp.float32), -6.0, 6.0)
    choose = jax.random.randint(second_key, (ATT_ROWS, HEADS), 0, 6, dtype=jnp.int32)
    strength = jnp.where(choose == 0, 8.0, jnp.where(choose == 1, 14.0, jnp.where(choose == 2, 20.0, 0.0)))
    aligned = strength[:, :, None] * signs[:, None, :]
    return jnp.where(strength[:, :, None] > 0.0, aligned, noise).astype(jnp.bfloat16)


def levels(own_key, extent, cuts, least, top_value):
    def one(dim, blocks):
        heights = jax.random.uniform(jax.random.fold_in(jax.random.fold_in(own_key, 6), dim), (blocks,), jnp.float32, least / len(cuts), top_value / len(cuts))
        return jnp.repeat(jnp.exp(heights), extent[dim] // blocks).reshape((-1,) + (1,) * (len(extent) - dim - 1))

    factor_of = one(*cuts[0])
    for cut in cuts[1:]:
        factor_of = factor_of * one(*cut)
    return factor_of


def assign_block(rng, own, number, rows, number_of, top, reach, skew):
    sequence = jax.random.permutation(rng, number_of)
    heavy_load, common = portions_of(number_of, rows * top, reach, skew, True), portions_of(number_of, rows * top, reach, skew, False)
    places = jnp.arange(number_of)

    def named(sizes, turn):
        used = int((sizes > 0).sum())
        fixed = max(1, used // 4)
        shifted = fixed + (places - fixed + turn * (used - fixed)) % max(1, number_of - fixed)
        return jnp.zeros((number_of,), jnp.int32).at[sequence[jnp.where(places < fixed, places, shifted)]].set(jnp.asarray(sizes, jnp.int32))

    sizes = jnp.where(number % 4 == 0, named(heavy_load, number // 4), named(common, number - number // 4 - 1))
    mixed = jax.random.permutation(jax.random.fold_in(own, 3), number_of)
    source_of, taker = mixed[0:number_of // 2 * 2:2], mixed[1:number_of // 2 * 2:2]
    room = jnp.minimum(sizes[source_of] - 1, reach - sizes[taker]) // 2
    room = jnp.where((source_of == sequence[0]) | (taker == sequence[0]) | (sizes[taker] == 0), 0, jnp.maximum(room, 0))
    shifted = jax.random.randint(jax.random.fold_in(own, 4), (number_of // 2,), 0, 1 << 20) % (room + 1)
    sizes = sizes.at[source_of].add(-shifted).at[taker].add(shifted)
    items = jnp.searchsorted(jnp.cumsum(sizes), jnp.arange(rows * top), side="right").astype(jnp.int32)
    grid = items.reshape(top, rows).T
    grid = grid[jax.random.permutation(jax.random.fold_in(own, 1), rows)]
    turn = jax.random.randint(jax.random.fold_in(own, 2), (rows, 1), 0, top)
    return jnp.take_along_axis(grid, (jnp.arange(top)[None, :] + turn) % top, axis=1)


def portions_of(amount, total, reach, slope, full):
    weights = [(1 << 20) // math.isqrt(grade ** slope) + 1 for grade in range(1, amount + 1)]
    largest = reach if full else min(reach, max(-(-total // amount), total * weights[0] // sum(weights)))
    least = 1 if total - largest >= amount - 1 else 0
    given, spare = [largest] + [least] * (amount - 1), total - largest - least * (amount - 1)
    while spare > 0:
        movable = [i for i in range(1, amount) if given[i] < largest] or [i for i in range(1, amount) if given[i] < reach]
        whole, left = sum([weights[i] for i in movable]), spare
        for i in movable:
            addition = min(reach - given[i], max(1, left * weights[i] // whole), spare)
            given[i] = given[i] + addition
            spare = spare - addition
    return np.array(given)


def scatter_about(stream_key, extent, deviation, limit, shards=(), kind=jnp.bfloat16):
    values = jax.random.normal(stream_key, extent, jnp.float32) * deviation
    if len(shards) > 0:
        values = levels(stream_key, extent, shards, -0.22, 0.18) * values
    return jnp.clip(values, min=-limit, max=limit).astype(kind)


def setup_inputs(seed: int = 0, part: int = 0) -> dict:
    streams_of = jax.random.split(jax.random.key(seed), 12)
    own_keys = jax.random.split(jax.random.fold_in(streams_of[11], part), 12)
    moe_input = scatter_about(own_keys[0], (MOE_ROWS, D), 1.0, 6.0, ((0, 32),))
    routes_keys = jax.random.split(jax.random.fold_in(own_keys[1], 1), MOE_ROWS // MOE_DEV)
    routes_turns = jax.random.permutation(jax.random.fold_in(own_keys[1], 3), MOE_ROWS // MOE_DEV)
    routes = jax.vmap(lambda own, number: assign_block(jax.random.fold_in(own_keys[1], 2), own, number, MOE_DEV, EXPERTS, TOPK, CAP, 2))(routes_keys, routes_turns).reshape((MOE_ROWS, TOPK))
    router_weight = scatter_about(streams_of[2], (D, EXPERTS), (D // 4) ** -0.5, 0.1875)
    gate_weight = scatter_about(streams_of[3], (EXPERTS, D, FF), D ** -0.5, 0.09375, ((0, 16), (2, 2)))
    up_weight = scatter_about(streams_of[4], (EXPERTS, D, FF), D ** -0.5, 0.09375, ((0, 16), (2, 2)))
    down_weight = scatter_about(streams_of[5], (EXPERTS, FF, D), FF ** -0.5, 0.1875, ((0, 16), (1, 2)))
    query_latent = draw_query_latent(jax.random.fold_in(jax.random.fold_in(streams_of[11], part), 71), part)
    query_rope = scatter_about(own_keys[7], (ATT_ROWS, ROPE, HEADS), 1.0, 6.0, ((0, 16),))
    cache_latent = draw_cache_latent(jax.random.fold_in(jax.random.fold_in(streams_of[11], part), 71), part)
    cache_rope = scatter_about(own_keys[9], (ATT_ROWS, ROPE, LEN), 1.0, 6.0, ((0, 16), (2, 2)))
    cache_lengths = draw_cache_lengths(jax.random.fold_in(jax.random.fold_in(streams_of[11], part), 71), part)
    return dict(moe_input=moe_input, routes=routes, router_weight=router_weight, gate_weight=gate_weight, up_weight=up_weight, down_weight=down_weight, query_latent=query_latent, query_rope=query_rope, cache_latent=cache_latent, cache_rope=cache_rope, cache_lengths=cache_lengths)


score_scale = 0.07216878364870323
route_scale = 2.5


def slot_tables(route_block, experts, capacity):
    entries, picks = route_block.shape
    flattened = route_block.reshape(entries * picks)
    expert_ids = jnp.arange(experts, dtype=jnp.int32)
    onehot = (flattened[:, None] == expert_ids[None, :]).astype(jnp.int32)
    earlier = jnp.cumsum(onehot, axis=0) - onehot
    position = jnp.sum(earlier * onehot, axis=1)
    target = flattened * capacity + position
    slot_ids = jnp.arange(experts * capacity, dtype=jnp.int32)
    select = (target[:, None] == slot_ids[None, :]).astype(jnp.float32)
    return select.reshape(entries, picks, experts * capacity), onehot.reshape(entries, picks, experts).astype(jnp.float32)


def expert_part(row_block, gate_slice, up_slice, down_slice):
    gate_value = jnp.dot(row_block, gate_slice, preferred_element_type=jnp.float32)
    up_value = jnp.dot(row_block, up_slice, preferred_element_type=jnp.float32)
    hidden = (jax.nn.silu(gate_value) * up_value).astype(jnp.bfloat16)
    return jnp.dot(hidden, down_slice, preferred_element_type=jnp.float32).astype(jnp.bfloat16)


def reference(moe_input, routes, router_weight, gate_weight, up_weight, down_weight, query_latent, query_rope, cache_latent, cache_rope, cache_lengths):
    pieces = N_TP * N_SUB
    slice_width = FF // pieces
    blocks = MOE_ROWS // MOE_DEV
    grouped = routes.reshape(blocks, MOE_DEV, TOPK)
    select, picked = jax.vmap(lambda block_routes: slot_tables(block_routes, EXPERTS, CAP))(grouped)
    logits = jnp.dot(moe_input, router_weight, preferred_element_type=jnp.float32)
    probs = jax.nn.sigmoid(logits).reshape(blocks, MOE_DEV, EXPERTS)
    chosen = jnp.sum(picked * probs[:, :, None, :], axis=3)
    gates = route_scale * chosen / jnp.sum(chosen, axis=2, keepdims=True)
    spread = jnp.sum(select, axis=2)
    weighting = jnp.sum(gates[:, :, :, None] * select, axis=2)
    row_blocks = moe_input.reshape(blocks, MOE_DEV, D).astype(jnp.float32)
    packed = jnp.einsum("brs,brd->bsd", spread, row_blocks, precision=lax.Precision.HIGHEST).astype(jnp.bfloat16)
    per_expert = packed.reshape(blocks, EXPERTS, CAP, D).transpose(1, 0, 2, 3).reshape(EXPERTS, blocks * CAP, D)

    def one_expert(items):
        gate_full, up_full, down_full, expert_rows = items
        running = jnp.zeros((expert_rows.shape[0], D), jnp.float32)
        for piece in range(pieces):
            lower = piece * slice_width
            part = expert_part(expert_rows, gate_full[:, lower:lower + slice_width], up_full[:, lower:lower + slice_width], down_full[lower:lower + slice_width, :])
            running = running + part.astype(jnp.float32)
        return running.astype(jnp.bfloat16)

    expert_out = lax.map(one_expert, (gate_weight, up_weight, down_weight, per_expert))
    expert_out = expert_out.reshape(EXPERTS, blocks, CAP, D).transpose(1, 0, 2, 3).reshape(blocks, EXPERTS * CAP, D)
    combined = jnp.einsum("brs,bsd->brd", weighting, expert_out.astype(jnp.float32), precision=lax.Precision.HIGHEST)
    moe_out = combined.astype(jnp.bfloat16).reshape(MOE_ROWS, D)

    positions = jnp.arange(LEN, dtype=jnp.int32)

    def one_row(items):
        query_lat, query_rot, cached_lat, cached_rot, length = items
        scores = jnp.dot(query_lat, cached_lat.T, preferred_element_type=jnp.float32)
        scores = (scores + jnp.dot(query_rot.T, cached_rot, preferred_element_type=jnp.float32)) * score_scale
        live = positions[None, :] < length
        masked = jnp.where(live, scores, -1e30)
        peak = jnp.max(masked, axis=1, keepdims=True)
        weights = jnp.where(live, jnp.exp(masked - peak), 0.0)
        denom = jnp.sum(weights, axis=1, keepdims=True)
        mixed = jnp.dot(weights.astype(jnp.bfloat16), cached_lat, preferred_element_type=jnp.float32)
        return (mixed / denom).astype(jnp.bfloat16)

    att_out = lax.map(one_row, (query_latent, query_rope, cache_latent, cache_rope, cache_lengths))
    return moe_out, att_out
```

```python
import jax
import jax.numpy as jnp
from jax import lax
from jax.sharding import PartitionSpec as P

score_scale = 0.07216878364870323
route_scale = 2.5
joint = ("wide", "tp", "sub")
lanes = 128


def log2(size):
    bits = size.bit_length() - 1
    assert 1 << bits == size
    return bits


def exchange_plan(wide, tp, sub):
    count = wide * tp * sub

    def flip(index, moves):
        parts = [index // (tp * sub), index // sub % tp, index % sub]
        for axis, bit in moves:
            parts[axis] ^= bit
        return (parts[0] * tp + parts[1]) * sub + parts[2]

    core = (2, 1) if sub > 1 else (0, 1)

    def parity(index):
        return (index % sub if sub > 1 else index // (tp * sub)) & 1

    moves = [(0, 1 << k) for k in reversed(range(log2(wide)))]
    moves += [(1, 1 << k) for k in reversed(range(log2(tp)))]
    moves += [(2, 1 << k) for k in reversed(range(log2(sub)))]
    moves = [m for m in moves if m != core]
    stages = []
    for first in range(0, len(moves), 2):
        group = moves[first : first + 2]
        if len(group) == 1:
            choices = [(group, group)]
        else:
            a, b = [group[0]], [group[1]]
            if group[0][0] == group[1][0]:
                choices = [(b, b), (a, a), (group, group)]
            else:
                choices = [(a, b), (b, a), (group, group)]
        stages.append(choices)
    stages.append([([core], [core])])
    return [
        [[(i, flip(i, pick[parity(i)])) for i in range(count)] for pick in choices]
        for choices in stages
    ]


def route_gates(moe_input, routes, router_weight, experts):
    logits = jnp.dot(moe_input, router_weight, preferred_element_type=jnp.float32)
    probs = jax.nn.sigmoid(logits)
    ids = jnp.arange(experts, dtype=jnp.int32)
    picked = jnp.any(routes[:, :, None] == ids[None, None, :], axis=1)
    chosen = jnp.where(picked, probs, 0.0)
    gates = route_scale * chosen / jnp.sum(chosen, axis=1, keepdims=True)
    upper = gates.astype(jnp.bfloat16)
    lower = (gates - upper.astype(jnp.float32)).astype(jnp.bfloat16)
    both = jnp.concatenate([upper, lower], axis=1)
    return jnp.pad(both, ((0, 0), (0, -both.shape[1] % lanes)))


def body(
    moe_input,
    routes,
    router_weight,
    gate_weight,
    up_weight,
    down_weight,
    query_latent,
    query_rope,
    cache_latent,
    cache_rope,
    cache_lengths,
):
    wide, tp, sub = (lax.axis_size(name) for name in joint)
    local_experts, width = gate_weight.shape[0], moe_input.shape[1]
    experts = wide * local_experts
    plan = exchange_plan(wide, tp, sub)

    def gather(piece, stage):
        return [piece] + [lax.ppermute(piece, joint, pairs) for pairs in stage]

    gates = route_gates(moe_input, routes, router_weight, experts)
    first = gather(moe_input, plan[0])
    first_gates = gather(gates, plan[0])
    rows = jnp.concatenate(
        [jnp.concatenate([a, b], axis=1) for a, b in zip(first, first_gates)], axis=0
    )
    for stage in plan[1:]:
        rows = jnp.concatenate(gather(rows, stage), axis=0)
    inputs, weights_all = rows[:, :width], rows[:, width:].astype(jnp.float32)
    columns = jnp.arange(weights_all.shape[1], dtype=jnp.int32)

    total = None
    for i in range(local_experts):
        gate_value = jnp.dot(inputs, gate_weight[i], preferred_element_type=jnp.float32)
        up_value = jnp.dot(inputs, up_weight[i], preferred_element_type=jnp.float32)
        hidden = (jax.nn.silu(gate_value) * up_value).astype(jnp.bfloat16)
        value = jnp.dot(hidden, down_weight[i], preferred_element_type=jnp.float32)
        expert = lax.axis_index("wide") * local_experts + i
        mine = (columns == expert) | (columns == expert + experts)
        weight = jnp.sum(jnp.where(mine[None, :], weights_all, 0.0), axis=1, keepdims=True)
        value = value * weight
        total = value if total is None else total + value

    local_len = cache_latent.shape[1]
    positions = lax.axis_index("tp") * local_len + jnp.arange(local_len, dtype=jnp.int32)
    scores = jnp.einsum(
        "rhc,rlc->rhl", query_latent, cache_latent, preferred_element_type=jnp.float32
    )
    scores = (
        scores
        + jnp.einsum("rkh,rkl->rhl", query_rope, cache_rope, preferred_element_type=jnp.float32)
    ) * score_scale
    live = positions[None, None, :] < cache_lengths[:, None, None]
    masked = jnp.where(live, scores, -1e30)
    peak = jnp.max(masked, axis=2)
    weights = jnp.where(live, jnp.exp(masked - peak[:, :, None]), 0.0)
    denom = jnp.sum(weights, axis=2)
    mixed = jnp.einsum(
        "rhl,rlc->rhc",
        weights.astype(jnp.bfloat16),
        cache_latent,
        preferred_element_type=jnp.float32,
    )

    def reduce(total, stage):
        parts = jnp.split(total, len(stage) + 1, axis=0)
        out = parts[0]
        for part, pairs in zip(parts[1:], stage):
            out = out + lax.ppermute(part.astype(jnp.bfloat16), joint, pairs).astype(jnp.float32)
        return out

    for stage in reversed(plan[1:]):
        total = reduce(total, stage)
    moe_out = reduce(total, plan[0]).astype(jnp.bfloat16)

    stats = jnp.stack([peak, denom])
    mixed_sent = mixed.astype(jnp.bfloat16)
    all_mixed, all_stats = [mixed], [stats]
    for step in range(1, tp):
        pairs = [(i, i ^ step) for i in range(tp)]
        all_mixed.append(lax.ppermute(mixed_sent, "tp", pairs).astype(jnp.float32))
        all_stats.append(lax.ppermute(stats, "tp", pairs))
    top = all_stats[0][0]
    for s in all_stats[1:]:
        top = jnp.maximum(top, s[0])
    above, below = 0.0, 0.0
    for m, s in zip(all_mixed, all_stats):
        factor = jnp.exp(s[0] - top)
        above = above + factor[:, :, None] * m
        below = below + factor * s[1]
    att_out = (above / below[:, :, None]).astype(jnp.bfloat16)
    return (moe_out, att_out)


def solution(mesh):
    in_specs = (
        P(("groups", "wide", "tp", "sub"), None),
        P(("groups", "wide", "tp", "sub"), None),
        P(),
        P("wide", None, ("tp", "sub")),
        P("wide", None, ("tp", "sub")),
        P("wide", ("tp", "sub"), None),
        P(("groups", "wide", "sub"), None, None),
        P(("groups", "wide", "sub"), None, None),
        P(("groups", "wide", "sub"), "tp", None),
        P(("groups", "wide", "sub"), None, "tp"),
        P(("groups", "wide", "sub")),
    )
    out_specs = (P(("groups", "wide", "tp", "sub"), None), P(("groups", "wide", "sub"), None, None))
    return jax.shard_map(body, mesh=mesh, in_specs=in_specs, out_specs=out_specs, check_vma=False)
```

```python
import functools

import jax
import jax.numpy as jnp
from jax import lax
from jax.experimental import pallas as pl
from jax.experimental.pallas import tpu as pltpu
from jax.sharding import PartitionSpec as P

score_scale = 0.07216878364870323
route_scale = 2.5
joint = ("wide", "tp", "sub")
lanes = 128


def log2(size):
    bits = size.bit_length() - 1
    assert 1 << bits == size
    return bits


def exchange_plan(wide, tp, sub):
    count = wide * tp * sub

    def flip(index, moves):
        parts = [index // (tp * sub), index // sub % tp, index % sub]
        for axis, bit in moves:
            parts[axis] ^= bit
        return (parts[0] * tp + parts[1]) * sub + parts[2]

    core = (2, 1) if sub > 1 else (0, 1)

    def parity(index):
        return (index % sub if sub > 1 else index // (tp * sub)) & 1

    moves = [(0, 1 << k) for k in reversed(range(log2(wide)))]
    moves += [(1, 1 << k) for k in reversed(range(log2(tp)))]
    moves += [(2, 1 << k) for k in reversed(range(log2(sub)))]
    moves = [m for m in moves if m != core]
    stages = []
    for first in range(0, len(moves), 2):
        group = moves[first : first + 2]
        if len(group) == 1:
            choices = [(group, group)]
        else:
            a, b = [group[0]], [group[1]]
            if group[0][0] == group[1][0]:
                choices = [(b, b), (a, a), (group, group)]
            else:
                choices = [(a, b), (b, a), (group, group)]
        stages.append(choices)
    stages.append([([core], [core])])
    return [
        [[(i, flip(i, pick[parity(i)])) for i in range(count)] for pick in choices]
        for choices in stages
    ]


VMEM = pl.BlockSpec(memory_space=pltpu.VMEM)
SMEM = pl.BlockSpec(memory_space=pltpu.SMEM)


def call(kernel, name, outs, in_specs, scratch=(), flops=0, moved=0, grant=8):
    shapes = [jax.ShapeDtypeStruct(shape, dtype) for shape, dtype in outs]
    return pl.pallas_call(
        kernel,
        out_shape=shapes,
        in_specs=in_specs,
        out_specs=[VMEM] * len(shapes),
        scratch_shapes=list(scratch),
        cost_estimate=pl.CostEstimate(flops=flops, bytes_accessed=moved, transcendentals=0),
        compiler_params=pltpu.CompilerParams(vmem_limit_bytes=grant << 20),
        name=name,
    )


def gates_kernel(x_ref, routes_ref, router_ref, out_ref):
    logits = lax.dot_general(
        x_ref[...], router_ref[...], (((1,), (1,)), ((), ())), preferred_element_type=jnp.float32
    )
    probs = jax.nn.sigmoid(logits)
    experts = probs.shape[1]
    routes = routes_ref[...]
    ids = lax.broadcasted_iota(jnp.int32, probs.shape, 1)
    chosen = jnp.zeros_like(probs)
    for k in range(routes.shape[1]):
        chosen = jnp.where(routes[:, k : k + 1] == ids, probs, chosen)
    gates = route_scale * chosen / jnp.sum(chosen, axis=1, keepdims=True)
    upper = gates.astype(jnp.bfloat16)
    lower = (gates - upper.astype(jnp.float32)).astype(jnp.bfloat16)
    shape = (experts, out_ref.shape[1] - x_ref.shape[1])
    row, lane = lax.broadcasted_iota(jnp.int32, shape, 0), lax.broadcasted_iota(jnp.int32, shape, 1)
    place = jnp.where(lane == row, 1.0, 0.0).astype(jnp.bfloat16)
    shift = jnp.where(lane == row + experts, 1.0, 0.0).astype(jnp.bfloat16)
    spread = jnp.dot(upper, place, preferred_element_type=jnp.float32)
    spread = spread + jnp.dot(lower, shift, preferred_element_type=jnp.float32)
    out_ref[:, : x_ref.shape[1]] = x_ref[...]
    out_ref[:, x_ref.shape[1] :] = spread.astype(jnp.bfloat16)


def stack_kernel(*refs):
    first = 0
    for ref in refs[:-1]:
        refs[-1][first : first + ref.shape[0], :] = ref[...]
        first += ref.shape[0]


def expert_kernel(pieces, experts, local_experts, first_ref, *refs):
    parts, (gate_ref, up_ref, down_ref, keep_ref, send_ref, rows_ref) = refs[:pieces], refs[pieces:]
    width = keep_ref.shape[1]
    half = keep_ref.shape[0]
    first, gates = 0, []
    for ref in parts:
        rows_ref[first : first + ref.shape[0], :] = ref[:, :width]
        gates.append(ref[:, width:].astype(jnp.float32))
        first += ref.shape[0]
    gates = jnp.concatenate(gates, axis=0)
    lane = lax.broadcasted_iota(jnp.int32, gates.shape, 1)
    block = 512 if width % 512 == 0 else width
    for i in range(local_experts):
        inputs = rows_ref[...]
        gate_value = jnp.dot(inputs, gate_ref[i], preferred_element_type=jnp.float32)
        up_value = jnp.dot(inputs, up_ref[i], preferred_element_type=jnp.float32)
        hidden = (gate_value / (1.0 + jnp.exp(-gate_value)) * up_value).astype(jnp.bfloat16)
        expert = first_ref[0] + i
        mine = (lane == expert) | (lane == expert + experts)
        weight = jnp.sum(jnp.where(mine, gates, 0.0), axis=1, keepdims=True)
        for low in range(0, width, block):
            value = jnp.dot(
                hidden, down_ref[i, :, low : low + block], preferred_element_type=jnp.float32
            )
            value = value * weight
            top, rest = value[:half], value[half:]
            if i > 0:
                top = top + keep_ref[:, low : low + block]
                rest = rest + send_ref[:, low : low + block].astype(jnp.float32)
            keep_ref[:, low : low + block] = top
            send_ref[:, low : low + block] = rest.astype(jnp.bfloat16)


def three_parts(value):
    first = value.astype(jnp.bfloat16).astype(jnp.float32)
    second = (value - first).astype(jnp.bfloat16).astype(jnp.float32)
    return first, second, value - first - second


def attend_kernel(live_ref, q_ref, qr_ref, k_ref, kr_ref, mixed_ref, stats_ref, send_ref, score_ref):
    length, width = k_ref.shape[1:]
    heads = q_ref.shape[1]
    block = 512 if length % 512 == 0 else length
    for r in range(q_ref.shape[0]):
        live = live_ref[r]
        query, turned = q_ref[r], qr_ref[r].T
        peak = jnp.full((heads, 1), -1e30, jnp.float32)
        for low in range(0, length, block):
            score = lax.dot_general(
                query,
                k_ref[r, low : low + block, :],
                (((1,), (1,)), ((), ())),
                preferred_element_type=jnp.float32,
            )
            score = score + jnp.dot(
                turned, kr_ref[r, :, low : low + block], preferred_element_type=jnp.float32
            )
            place = low + lax.broadcasted_iota(jnp.int32, score.shape, 1)
            score = jnp.where(place < live, score * score_scale, -1e30)
            score_ref[:, low : low + block] = score
            peak = jnp.maximum(peak, jnp.max(score, axis=1, keepdims=True))
        denom = jnp.zeros((heads, 1), jnp.float32)
        mixed = jnp.zeros((heads, width), jnp.float32)
        for low in range(0, length, block):
            score = score_ref[:, low : low + block]
            place = low + lax.broadcasted_iota(jnp.int32, score.shape, 1)
            weight = jnp.where(place < live, jnp.exp(score - peak), 0.0)
            denom = denom + jnp.sum(weight, axis=1, keepdims=True)
            mixed = mixed + jnp.dot(
                weight.astype(jnp.bfloat16),
                k_ref[r, low : low + block, :],
                preferred_element_type=jnp.float32,
            )
        mixed_ref[r] = mixed
        send_ref[r, :, :width] = mixed.astype(jnp.bfloat16)
        lane = lax.broadcasted_iota(jnp.int32, (heads, lanes), 1)
        packed = jnp.zeros((heads, lanes), jnp.float32)
        for i, part in enumerate(three_parts(peak) + three_parts(denom)):
            packed = jnp.where(lane == i, part, packed)
        send_ref[r, :, width:] = packed.astype(jnp.bfloat16)
        stats_ref[r] = jnp.where(lane == 0, peak, jnp.where(lane == 1, denom, 0.0))


def meet_kernel(mixed_ref, stats_ref, *refs):
    others, out_ref = refs[:-1], refs[-1]
    width = mixed_ref.shape[2]
    for r in range(mixed_ref.shape[0]):
        peaks, sums = [stats_ref[r, :, 0:1]], [stats_ref[r, :, 1:2]]
        mixes = [mixed_ref[r]]
        for ref in others:
            stats = ref[r, :, width:].astype(jnp.float32)
            peaks.append(stats[:, 0:1] + stats[:, 1:2] + stats[:, 2:3])
            sums.append(stats[:, 3:4] + stats[:, 4:5] + stats[:, 5:6])
            mixes.append(ref[r, :, :width].astype(jnp.float32))
        top = functools.reduce(jnp.maximum, peaks)
        above, below = 0.0, 0.0
        for peak, total, mixed in zip(peaks, sums, mixes):
            factor = jnp.exp(peak - top)
            above = above + factor * mixed
            below = below + factor * total
        out_ref[r] = (above / below).astype(jnp.bfloat16)


def body(
    moe_input,
    routes,
    router_weight,
    gate_weight,
    up_weight,
    down_weight,
    query_latent,
    query_rope,
    cache_latent,
    cache_rope,
    cache_lengths,
):
    wide, tp, sub = (lax.axis_size(name) for name in joint)
    local_experts, width, hidden = gate_weight.shape
    experts = wide * local_experts
    own_rows = moe_input.shape[0]
    plan = exchange_plan(wide, tp, sub)
    bf16, f32 = jnp.bfloat16, jnp.float32

    def gather(piece, stage):
        return [piece] + [lax.ppermute(piece, joint, pairs) for pairs in stage]

    extra = 2 * experts + -2 * experts % lanes
    (piece,) = call(gates_kernel, "gates", [((own_rows, width + extra), bf16)], [VMEM] * 3)(
        moe_input, routes, router_weight.T
    )
    pieces, held = [piece], own_rows
    for stage in plan[:-1]:
        if len(pieces) > 1:
            (piece,) = call(
                stack_kernel, "stack", [((held, width + extra), bf16)], [VMEM] * len(pieces)
            )(*pieces)
        pieces = gather(piece, stage)
        held *= len(pieces)
    pieces = pieces + [lax.ppermute(p, joint, plan[-1][0]) for p in pieces]

    first_expert = (lax.axis_index("wide") * local_experts).reshape(1).astype(jnp.int32)
    total, sent = call(
        functools.partial(expert_kernel, len(pieces), experts, local_experts),
        "expert",
        [((held, width), f32), ((held, width), bf16)],
        [SMEM] + [VMEM] * (len(pieces) + 3),
        scratch=[pltpu.VMEM((2 * held, width), bf16)],
        flops=12 * held * width * hidden * local_experts,
        moved=6 * width * hidden * local_experts,
        grant=24,
    )(first_expert, *pieces, gate_weight, up_weight, down_weight)

    rows, heads, latent = query_latent.shape
    local_len = cache_latent.shape[1]
    live = cache_lengths - lax.axis_index("tp").astype(jnp.int32) * local_len
    mixed, stats, mixed_sent = call(
        attend_kernel,
        "attend",
        [
            ((rows, heads, latent), f32),
            ((rows, heads, lanes), f32),
            ((rows, heads, latent + lanes), bf16),
        ],
        [SMEM] + [VMEM] * 4,
        scratch=[pltpu.VMEM((heads, local_len), f32)],
        flops=4 * rows * heads * local_len * latent,
        moved=2 * rows * local_len * latent,
    )(live, query_latent, query_rope, cache_latent, cache_rope)
    others = [
        lax.ppermute(mixed_sent, "tp", [(i, i ^ step) for i in range(tp)]) for step in range(1, tp)
    ]
    (att_out,) = call(
        meet_kernel, "meet", [((rows, heads, latent), bf16)], [VMEM] * (2 + len(others))
    )(mixed, stats, *others)

    total = total + lax.ppermute(sent, joint, plan[-1][0]).astype(f32)
    for stage in reversed(plan[:-1]):
        parts = jnp.split(total, len(stage) + 1, axis=0)
        total = parts[0]
        for part, pairs in zip(parts[1:], stage):
            total = total + lax.ppermute(part.astype(bf16), joint, pairs).astype(f32)
    return (total.astype(bf16), att_out)


def solution(mesh):
    in_specs = (
        P(("groups", "wide", "tp", "sub"), None),
        P(("groups", "wide", "tp", "sub"), None),
        P(),
        P("wide", None, ("tp", "sub")),
        P("wide", None, ("tp", "sub")),
        P("wide", ("tp", "sub"), None),
        P(("groups", "wide", "sub"), None, None),
        P(("groups", "wide", "sub"), None, None),
        P(("groups", "wide", "sub"), "tp", None),
        P(("groups", "wide", "sub"), None, "tp"),
        P(("groups", "wide", "sub")),
    )
    out_specs = (P(("groups", "wide", "tp", "sub"), None), P(("groups", "wide", "sub"), None, None))
    return jax.shard_map(body, mesh=mesh, in_specs=in_specs, out_specs=out_specs, check_vma=False)
```
